32 devices in a mesh: node: 8 (over z, x), feat: 4 (over y, core).
Axes of the slice: x: 2, y: 2, z: 4, core: 2. Of those that a mesh axis runs over, the one named last changes fastest.
Arguments:
- feature_table: bfloat16 [8192, 2048], P('node', 'feat'), may hold values from -6 to 6
- hub_table: bfloat16 [32, 2048], P('node', 'feat'), may hold values from -6 to 6
- first_self: bfloat16 [2048, 2048], P('feat'), may hold values from -0.125 to 0.125
- first_pooled: bfloat16 [2048, 2048], P('feat'), may hold values from -0.125 to 0.125
- second_self: bfloat16 [2048, 256], P('feat'), may hold values from -0.125 to 0.125
- second_pooled: bfloat16 [2048, 256], P('feat'), may hold values from -0.125 to 0.125
- first_lists: int32 [3072, 10], P('node'), may hold values from 0 to 8223, as said below
- first_counts: int32 [3072], P('node'), may hold values from 1 to 10
- second_lists: int32 [2048, 5], P('node'), may hold values from 0 to 3071, as said below
- second_counts: int32 [2048], P('node'), may hold values from 1 to 5
Outputs:
- embedding: bfloat16 [2048, 256], P(('node', 'feat'))
The draws below stay inside these ranges and needn't reach their ends.
Inputs may be any that keep to these rules, and one draw needn't show every extreme that they name: `first_lists`: an entry below 8192 names a row of feature_table, held by node shard (entry // 1024); an entry v of 8192 or more names hub clip v - 8192, owned by node shard (v - 8192) // 4. Slots at or beyond a clip's count are padding and still hold such entries. Of the 3840 entries of one node shard's rows, padding included, at most 480 name feature rows held by any one node shard; in every draw one node shard is named exactly 480 times by the rows of every node shard. `second_lists`: entries name frontier clips, held by node shard (entry // 384). Of the 1280 entries of one node shard's rows, padding included, exactly 160 name frontier clips of each node shard.
All inputs are finite; a program needn't handle non-finite values.
Results may differ from the reference program's by a relative error of at most 0.0052.
Values may be sent and summed in bfloat16 or wider, within the bound.
A program may use at most 64 MiB of HBM per device.

```python
import jax
import jax.numpy as jnp
from jax import lax

F = 2048
H = 2048
O = 256
FAN1 = 10
FAN2 = 5
ROWS_DEV = 1024
FRONT_DEV = 384
TGT_DEV = 256
NROWS = 8192
HUBS = 32
FRONT = 3072
TARGETS = 2048
CAP1 = 480
CAP2 = 160
N_NODE = 8
N_FEAT = 4


def draw_first_lists(key, part):
    shards = NROWS // ROWS_DEV
    slots = FRONT_DEV * FAN1
    keys = jax.random.split(jax.random.fold_in(key, 11), 7)
    levels = jax.random.randint(keys[0], (shards, shards), 1, 9)
    favoured = jax.random.randint(keys[1], (), 0, shards)
    columns = jnp.arange(shards, dtype=jnp.int32)[None, :]
    levels = jnp.where(columns == favoured, 8, levels)
    second_full = jax.random.randint(keys[2], (shards, 1), 0, shards)
    levels = jnp.where(columns == second_full, 8, levels)
    owner = jnp.arange(slots, dtype=jnp.int32) // CAP1
    coin = jax.random.randint(keys[3], (shards, slots), 0, 8)
    live = coin < jnp.take(levels, owner, axis=1)
    drawn = jax.random.randint(keys[4], (shards, slots), 0, ROWS_DEV) + owner[None, :] * ROWS_DEV
    hubward = NROWS + jax.random.randint(keys[5], (shards, slots), 0, HUBS)
    entries = jnp.where(live, drawn, hubward)
    rows_index = jnp.arange(shards, dtype=jnp.int32)[:, None]
    slot_index = jnp.arange(slots, dtype=jnp.int32)[None, :]
    entries = jnp.where((rows_index == 0) & (slot_index == 0), 0, entries)
    other_owner = (favoured + 1) % shards
    top_slot = other_owner * CAP1 + CAP1 - 1
    entries = jnp.where((rows_index == 0) & (slot_index == top_slot), NROWS + HUBS - 1, entries)
    shuffle_keys = jax.random.split(keys[6], shards)
    order = jax.vmap(lambda one_key: jax.random.permutation(one_key, slots))(shuffle_keys)
    entries = jnp.take_along_axis(entries, order, axis=1)
    return entries.reshape(shards * FRONT_DEV, FAN1).astype(jnp.int32)


def draw_second_lists(key, part):
    shards = NROWS // ROWS_DEV
    slots = TGT_DEV * FAN2
    choose_key, shuffle_key = jax.random.split(jax.random.fold_in(key, 31))
    owner = jnp.arange(slots, dtype=jnp.int32) // CAP2
    picks = jax.random.randint(choose_key, (shards, slots), 0, FRONT_DEV) + owner[None, :] * FRONT_DEV
    rows_index = jnp.arange(shards, dtype=jnp.int32)[:, None]
    slot_index = jnp.arange(slots, dtype=jnp.int32)[None, :]
    picks = jnp.where((rows_index == 0) & (slot_index == 0), 0, picks)
    picks = jnp.where((rows_index == 0) & (slot_index == slots - 1), shards * FRONT_DEV - 1, picks)
    shuffle_keys = jax.random.split(shuffle_key, shards)
    order = jax.vmap(lambda one_key: jax.random.permutation(one_key, slots))(shuffle_keys)
    picks = jnp.take_along_axis(picks, order, axis=1)
    return picks.reshape(shards * TGT_DEV, FAN2).astype(jnp.int32)


def count_draw(key, salt, total, fanout):
    coin_key, value_key = jax.random.split(jax.random.fold_in(key, salt))
    values = jax.random.randint(value_key, (total,), 1, fanout + 1)
    coin = jax.random.randint(coin_key, (total,), 0, 5)
    counts = jnp.where(coin < 3, fanout, values)
    position = jnp.arange(total, dtype=jnp.int32)
    counts = jnp.where(position == 0, fanout, counts)
    counts = jnp.where(position == 1, 1, counts)
    return counts.astype(jnp.int32)


def draw_first_counts(key, part):
    return count_draw(key, 41, NROWS // ROWS_DEV * FRONT_DEV, FAN1)


def draw_second_counts(key, part):
    return count_draw(key, 43, NROWS // ROWS_DEV * TGT_DEV, FAN2)


def block_scale(own_key, shape, cuts, low, top_value):
    level = 1.0
    for axis_at, blocks in cuts:
        heights = jax.random.uniform(jax.random.fold_in(jax.random.fold_in(own_key, 6), axis_at), (blocks,), jnp.float32, low / len(cuts), top_value / len(cuts))
        level = level * jnp.repeat(jnp.exp(heights), shape[axis_at] // blocks).reshape((-1,) + (1,) * (len(shape) - 1 - axis_at))
    return level


def gaussian(rng, shape, scale, most, pieces=(), kind=jnp.bfloat16):
    drawn = jax.random.normal(rng, shape, jnp.float32) * scale
    if len(pieces) > 0:
        drawn = block_scale(rng, shape, pieces, -0.22, 0.18) * drawn
    return jnp.clip(drawn, min=-most, max=most).astype(kind)


def setup_inputs(seed: int = 0) -> dict:
    streams_of = jax.random.split(jax.random.key(seed), 11)
    feature_table = gaussian(streams_of[0], (NROWS, F), 1.0, 6.0, ((0, 8), (1, 4)))
    hub_table = gaussian(streams_of[1], (HUBS, F), 1.0, 6.0, ((0, 8), (1, 4)))
    first_self = gaussian(streams_of[2], (F, H), F ** -0.5, 0.125, ((0, 4),))
    first_pooled = gaussian(streams_of[3], (F, H), F ** -0.5, 0.125, ((0, 4),))
    second_self = gaussian(streams_of[4], (H, O), H ** -0.5, 0.125, ((0, 4),))
    second_pooled = gaussian(streams_of[5], (H, O), H ** -0.5, 0.125, ((0, 4),))
    first_lists = draw_first_lists(jax.random.fold_in(streams_of[10], 71), 0)
    first_counts = draw_first_counts(jax.random.fold_in(streams_of[10], 71), 0)
    second_lists = draw_second_lists(jax.random.fold_in(streams_of[10], 71), 0)
    second_counts = draw_second_counts(jax.random.fold_in(streams_of[10], 71), 0)
    return dict(feature_table=feature_table, hub_table=hub_table, first_self=first_self, first_pooled=first_pooled, second_self=second_self, second_pooled=second_pooled, first_lists=first_lists, first_counts=first_counts, second_lists=second_lists, second_counts=second_counts)


def first_block(shard, pooled, feature_table, self_split, pool_split, first_lists, first_counts):
    begin = (shard * FRONT_DEV).astype(jnp.int32)
    lists = lax.dynamic_slice_in_dim(first_lists, begin, FRONT_DEV, 0)
    counts = lax.dynamic_slice_in_dim(first_counts, begin, FRONT_DEV, 0)
    picked = jnp.take(pooled, lists, axis=0).astype(jnp.float32)
    valid = jnp.arange(FAN1, dtype=jnp.int32)[None, :] < counts[:, None]
    summed = lax.optimization_barrier(jnp.sum(jnp.where(valid[:, :, None], picked, jnp.float32(0.0)), axis=1))
    first_mean = (summed / counts[:, None].astype(jnp.float32)).astype(jnp.bfloat16)
    own_rows = lax.dynamic_slice_in_dim(feature_table, (shard * ROWS_DEV).astype(jnp.int32), FRONT_DEV, 0)
    group = F // N_FEAT
    own_split = own_rows.astype(jnp.float32).reshape(FRONT_DEV, N_FEAT, group)
    mean_split = first_mean.astype(jnp.float32).reshape(FRONT_DEV, N_FEAT, group)
    parts = jnp.einsum('rgc,gch->grh', own_split, self_split, precision=lax.Precision.HIGHEST)
    parts = parts + jnp.einsum('rgc,gch->grh', mean_split, pool_split, precision=lax.Precision.HIGHEST)
    return jax.nn.relu(lax.optimization_barrier(jnp.sum(parts, axis=0))).astype(jnp.bfloat16)

def second_block(shard, hidden, second_self, second_pooled, second_lists, second_counts):
    begin = (shard * TGT_DEV).astype(jnp.int32)
    lists = lax.dynamic_slice_in_dim(second_lists, begin, TGT_DEV, 0)
    counts = lax.dynamic_slice_in_dim(second_counts, begin, TGT_DEV, 0)
    picked = jnp.take(hidden, lists, axis=0).astype(jnp.float32)
    valid = jnp.arange(FAN2, dtype=jnp.int32)[None, :] < counts[:, None]
    summed = lax.optimization_barrier(jnp.sum(jnp.where(valid[:, :, None], picked, jnp.float32(0.0)), axis=1))
    second_mean = (summed / counts[:, None].astype(jnp.float32)).astype(jnp.bfloat16)
    own_hidden = lax.dynamic_slice_in_dim(hidden, (shard * FRONT_DEV).astype(jnp.int32), TGT_DEV, 0)
    mixed = jnp.dot(own_hidden, second_self, preferred_element_type=jnp.float32)
    mixed = mixed + jnp.dot(second_mean, second_pooled, preferred_element_type=jnp.float32)
    scale = lax.rsqrt(lax.optimization_barrier(jnp.mean(mixed * mixed, axis=1, keepdims=True)) + 1e-06)
    return (mixed * scale).astype(jnp.bfloat16)

def reference(feature_table, hub_table, first_self, first_pooled, second_self, second_pooled, first_lists, first_counts, second_lists, second_counts):
    pooled = jnp.concatenate([feature_table, hub_table], axis=0)
    group = F // N_FEAT
    self_split = first_self.astype(jnp.float32).reshape(N_FEAT, group, H)
    pool_split = first_pooled.astype(jnp.float32).reshape(N_FEAT, group, H)
    shards = jnp.arange(N_NODE, dtype=jnp.int32)
    hidden = lax.map(lambda shard: first_block(shard, pooled, feature_table, self_split, pool_split, first_lists, first_counts), shards)
    hidden = hidden.reshape(FRONT, H)
    embedding = lax.map(lambda shard: second_block(shard, hidden, second_self, second_pooled, second_lists, second_counts), shards)
    return embedding.reshape(TARGETS, O)
```

```python
import functools
import types

import jax
import jax.numpy as jnp
from jax import lax
from jax.experimental import pallas as pl
from jax.experimental.pallas import tpu as pltpu
from jax.sharding import PartitionSpec as P

MESH = pl.DeviceIdType.MESH
CORES = 2
LANES = 128
TILES = 4
HUB_ROWS = 16
LIST_ROWS = 16


def greet(peers):
    barrier = pltpu.get_barrier_semaphore()
    for peer in peers:
        pl.semaphore_signal(barrier, inc=1, device_id=peer, device_id_type=MESH)
    pl.semaphore_wait(barrier, len(peers))


def remote(src, dst, sends, recvs, peer):
    return pltpu.make_async_remote_copy(
        src_ref=src, dst_ref=dst, send_sem=sends, recv_sem=recvs, device_id=peer, device_id_type=MESH
    )


def count_tiles(local, fan, names, store):
    rows = local.shape[0]
    local = local.astype(jnp.int16)
    one, zero = jnp.bfloat16(1), jnp.bfloat16(0)
    picked = [jnp.broadcast_to(local[:, k : k + 1], (rows, LANES)) for k in range(fan)]
    for at, columns in enumerate(names):
        columns = columns(rows)
        total = jnp.zeros((rows, LANES), jnp.bfloat16)
        for k in range(fan):
            total = total + jnp.where(picked[k] == columns, one, zero)
        store(at * LANES, total)


def plain_names(base, count):
    def name(start, rows):
        return (lax.broadcasted_iota(jnp.int32, (rows, LANES), 1) + start).astype(jnp.int16)

    return [functools.partial(name, base + at * LANES) for at in range(count)]


def main_kernel(d, names, *refs):
    r = types.SimpleNamespace(**dict(zip(names, refs)))
    f32, bf16 = jnp.float32, jnp.bfloat16
    node, feat = lax.axis_index("node"), lax.axis_index("feat")
    z, x = node // d.big_x, lax.rem(node, d.big_x)
    y, core = feat // CORES, lax.rem(feat, CORES)
    other = 1 - core
    place = core * d.big_y + y
    x_peers = [{"node": z * d.big_x + lax.rem(x + o, d.big_x)} for o in range(1, d.big_x)]
    y_peers = [{"feat": lax.rem(y + o, d.big_y) * CORES + core} for o in range(1, d.big_y)]
    n_peers = [{"node": lax.rem(node + o, d.shards)} for o in range(1, d.shards)]
    f_peers = [{"feat": lax.rem(feat + o, d.feats)} for o in range(1, d.feats)]
    c_peer = {"feat": y * CORES + other}

    def z_peer(to):
        return {"node": to * d.big_x + x}

    my_rows = pl.ds(pl.multiple_of(x * d.rows, d.rows), d.rows)
    my_units = pl.ds(pl.multiple_of(feat * d.hidden_part, d.hidden_part), d.hidden_part)
    loads = [
        pltpu.make_async_copy(r.table, r.tables.at[my_rows], r.load.at[0]),
        pltpu.make_async_copy(r.self_one, r.w_self, r.load.at[1]),
        pltpu.make_async_copy(r.pool_one, r.w_pool, r.load.at[2]),
        pltpu.make_async_copy(r.self_two, r.v_self.at[my_units], r.load.at[3]),
        pltpu.make_async_copy(r.pool_two, r.v_pool.at[my_units], r.load.at[4]),
    ]
    for copy in loads:
        copy.start()
    hub_top = d.big_x * d.rows
    r.hubs[...] = jnp.zeros(r.hubs.shape, bf16)
    r.hubs[0 : d.hubs_here, :] = r.hub[...]
    r.tables[hub_top : d.depth, :] = jnp.zeros((d.depth - hub_top, d.width), bf16)
    my_hubs = pl.ds(pl.multiple_of(hub_top + x * HUB_ROWS, HUB_ROWS), HUB_ROWS)
    r.tables[my_hubs, :] = r.hubs[...]
    greet(n_peers + f_peers)

    def x_copy(h, o):
        cut = pl.ds(h * LANES, LANES)
        return remote(
            r.table.at[:, cut], r.tables.at[my_rows, cut], r.x_ss.at[h, o], r.x_rs.at[h, o], x_peers[o]
        )


    def h_copy(o):
        return remote(r.hubs, r.tables.at[my_hubs], r.h_ss.at[o], r.h_rs.at[o], x_peers[o])

    for o in range(d.big_x - 1):
        h_copy(o).start()
        x_copy(0, o).start()

    line = lax.broadcasted_iota(jnp.int32, (LIST_ROWS, d.front), 0)
    r.raw[...] = jnp.full((LIST_ROWS, d.front), -1, jnp.int32)
    r.raw[0 : d.fan_one, :] = r.lists_one[...]
    counts = jnp.broadcast_to(r.counts_one[...], (LIST_ROWS, d.front))
    entry = jnp.where(line < jnp.minimum(counts, d.fan_one), r.raw[...], -1)

    def decode(to):
        here = entry - to * (d.big_x * d.rows)
        found = jnp.where((here >= 0) & (here < hub_top), here, -1)
        for slot in range(d.big_x):
            hub = entry - (d.shards * d.rows + (to * d.big_x + slot) * d.hubs_here)
            found = jnp.where(
                (hub >= 0) & (hub < d.hubs_here), hub + (hub_top + slot * HUB_ROWS), found
            )
        return found

    def l_copy(o):
        to = lax.rem(z + o, d.big_z)
        return remote(
            r.l_send.at[o - 1], r.l_recv.at[z], r.l_ss.at[o - 1], r.l_rs.at[o - 1], z_peer(to)
        )

    for o in range(1, d.big_z):
        r.l_send[o - 1] = decode(lax.rem(z + o, d.big_z)).astype(jnp.int16)
        l_copy(o).start()

    def place_rows(slot, found):
        turned = found.T
        for to, start, _ in d.order:
            r.local[slot, to : to + d.step, :] = turned[start : start + d.step, :]

    own_slot = d.big_z - 1
    place_rows(own_slot, jnp.where(line == d.fan_one, counts, decode(z)))

    line_two = lax.broadcasted_iota(jnp.int32, (8, d.targets), 0)
    counts_two = jnp.broadcast_to(r.counts_two[...], (8, d.targets))
    r.raw_two[...] = jnp.full((8, d.targets), -1, jnp.int32)
    r.raw_two[0 : d.fan_two, :] = r.lists_two[...]
    second = jnp.where(line_two < jnp.minimum(counts_two, d.fan_two), r.raw_two[...], -1)
    second = jnp.where(line_two == d.fan_two, counts_two, second)
    r.s_send[...] = second
    r.s_recv[node] = second

    def s_copy(o):
        return remote(r.s_send, r.s_recv.at[node], r.s_ss.at[o], r.s_rs.at[o], n_peers[o])

    for o in range(d.shards - 1):
        s_copy(o).start()

    for h in range(1, d.chunks):
        for o in range(d.big_x - 1):
            x_copy(h, o).start()

    def v_copies(o):
        return [
            remote(r.self_two, r.v_self.at[my_units], r.v_ss.at[0, o], r.v_rs.at[0, o], f_peers[o]),
            remote(r.pool_two, r.v_pool.at[my_units], r.v_ss.at[1, o], r.v_rs.at[1, o], f_peers[o]),
        ]

    for o in range(d.feats - 1):
        for copy in v_copies(o):
            copy.start()

    own_rows = pl.ds(pl.multiple_of(x * d.rows, d.rows), d.front)

    def own_part(j, carry):
        cut = pl.ds(pl.multiple_of(j * d.tile, LANES), d.tile)
        value = jnp.dot(r.tables[own_rows, :], r.w_self[:, cut], preferred_element_type=f32)
        for to, start, _ in d.order:
            r.part[j, to : to + d.step, :] = value[start : start + d.step, :]
        return carry

    turn = 2 * z // d.big_z

    turns = max(d.big_z - 1, 1)

    def target_of(s):
        mirrored = z + turn * (d.big_z - 1 - 2 * z)
        back = (s + mirrored) // turns
        to = (1 - back) * (d.big_z - 1 - s) + back * (s + mirrored - turns)
        return to + turn * (d.big_z - 1 - 2 * to)

    for o in range(1, d.big_z):
        l_copy(o).wait()

    def take_list(s, carry):
        place_rows(s, r.l_recv[target_of(s)].astype(jnp.int32))
        return carry

    lax.fori_loop(0, d.big_z - 1, take_list, 0)

    tile_names = plain_names(0, d.depth // LANES)

    def fill(slot):
        def group(i, carry):
            row0 = pl.multiple_of(i * 32, 32)

            def store(start, value):
                r.matrix[slot, pl.ds(row0, 32), start : start + LANES] = value

            count_tiles(r.local[slot, pl.ds(row0, 32), :], d.fan_one, tile_names, store)
            return carry

        lax.fori_loop(0, d.front // 32, group, 0)

    last = d.chunks - 1
    block = d.feats * d.step
    split = [h for h in (last - 1, last) if h > 0 or h == last]
    pieces = [(0, d.front, h) for h in range(split[0])]
    whole = len(pieces)
    piece_of = {}
    for group in (range(d.blocks - 1), (d.blocks - 1,)):
        for h in split:
            for q in group:
                piece_of[q, h] = len(pieces)
                pieces.append((q * block, block, h))
    odd = lax.rem(z, 2)
    partner = z + 1 - 2 * odd

    def region(p):
        top, deep, h = pieces[p]
        return pl.ds(top, deep), pl.ds(h * LANES, LANES)

    def held(s):
        to = target_of(s)
        return ((odd == 1) & (to > z)) | ((odd == 0) & (to < z))

    def led(s):
        to = target_of(s)
        return ((odd == 0) & (to > z + 1)) | ((odd == 1) & (to < z - 1))

    def hop_copy(s, p, slot, peer):
        rows, cut = region(p)
        return remote(
            r.z_send.at[s, rows, cut],
            r.z_recv.at[slot, rows, cut],
            r.z_ss.at[s, p],
            r.z_rs.at[slot, p],
            z_peer(peer),
        )

    def led_copy(s, p):
        return hop_copy(s, p, d.big_z + target_of(s), partner)

    def final_copy(s, p):
        return hop_copy(s, p, z, target_of(s))

    def arrival(slot, p):
        rows, cut = region(p)
        at = r.z_recv.at[slot, rows, cut]
        return remote(at, at, r.z_rs.at[slot, p], r.z_rs.at[slot, p], z_peer(lax.rem(z + 1, d.big_z)))

    def relay(p):
        top, deep, h = pieces[p]
        rows = slice(top, top + deep)
        cut = slice(h * LANES, (h + 1) * LANES)

        def one(s, carry):
            @pl.when(held(s))
            def _():
                slot = d.big_z + target_of(s)
                arrival(slot, p).wait_recv()
                r.z_send[s, rows, cut] = (
                    r.hold[s, rows, cut] + r.z_recv[slot, rows, cut].astype(f32)
                ).astype(bf16)
                final_copy(s, p).start()

            return carry

        lax.fori_loop(0, d.big_z - 1, one, 0)

    def sums(h, s):
        cut = slice(h * LANES, (h + 1) * LANES)
        value = jnp.dot(r.matrix[s], r.tables[:, cut], preferred_element_type=f32)

        kept = held(s)

        @pl.when(kept)
        def _():
            r.hold[s, :, cut] = value

        @pl.when(jnp.logical_not(kept))
        def _():
            r.z_send[s, :, cut] = value.astype(bf16)

    def launch(s, p):
        @pl.when(led(s))
        def _():
            led_copy(s, p).start()

        @pl.when(jnp.logical_not(held(s) | led(s)))
        def _():
            final_copy(s, p).start()

    def send_all(ps):
        for p in ps:
            for s in range(d.big_z - 1):
                launch(s, p)

    def chunk(h):
        for o in range(d.big_x - 1):
            x_copy(h, o).wait()

        def one_target(s, carry):
            sums(h, s)
            if h < split[0]:
                launch(s, h)
            return carry

        lax.fori_loop(0, d.big_z - 1, one_target, 0)

    relayed = set()

    def relays(p):
        if d.big_z > 2 and p not in relayed:
            relayed.add(p)

            relay(p)

    def fill_second(n, carry):
        local = (r.s_recv[n]).T
        r.turned[...] = local
        mine = r.turned[pl.ds(pl.multiple_of(feat * d.piece, 8), d.piece), :]
        row = pl.multiple_of(n * d.piece, 16)

        def store(start, value):
            r.matrix_two[pl.ds(row, d.piece), start : start + LANES] = value

        found = jnp.clip(mine[:, 0 : d.fan_two] - node * d.front, -1, d.front)
        count_tiles(found, d.fan_two, second_names, store)
        r.scale_two[pl.ds(row, d.piece), :] = 1.0 / mine[:, d.fan_two : d.fan_two + 1].astype(f32)
        return carry

    def second_name(start, rows):
        lane = lax.broadcasted_iota(jnp.int32, (rows, LANES), 1) + start
        q = lane // block
        rest = lane - q * block
        spot = rest // d.step
        within = rest - spot * d.step
        c = spot // d.big_y
        f = (spot - c * d.big_y) * CORES + c
        early = d.targets + f * d.step + within
        late = f * d.piece + (q - 1) * d.step + within
        return jnp.where(q == 0, early, late).astype(jnp.int16)

    second_names = [functools.partial(second_name, at) for at in range(0, d.front, LANES)]

    fill(0)
    if d.big_z > 2:
        fill(1)
    for o in range(d.big_x - 1):
        x_copy(0, o).wait()
        h_copy(o).wait()
    loads[0].wait()

    def first_sums(s, carry):
        @pl.when(s > 1)
        def _():
            fill(s)

        sums(0, s)
        if split[0] > 0:
            launch(s, 0)
        return carry

    lax.fori_loop(0, d.big_z - 1, first_sums, 0)
    loads[1].wait()
    lax.fori_loop(0, TILES, own_part, 0)
    for h in range(1, d.chunks):
        if h < last - 1:
            relays(h - 1)
        chunk(h)
        if h == last - 1:
            if h > 0:
                send_all([piece_of[q, h] for q in range(d.blocks - 1)])
            if h - 1 >= 0 and split[0] > h - 1:
                relays(h - 1)
        if h == max(last - 2, 1):
            for o in range(d.shards - 1):
                s_copy(o).wait()
            lax.fori_loop(0, d.shards, fill_second, 0)
        if h == last - 1:
            fill(own_slot)
    if last <= 1:
        if last == 0:
            for o in range(d.shards - 1):
                s_copy(o).wait()
            lax.fori_loop(0, d.shards, fill_second, 0)
        fill(own_slot)
        send_all(range(whole, len(pieces)))
    else:
        send_all([piece_of[q, last] for q in range(d.blocks - 1)])
        send_all([piece_of[d.blocks - 1, h] for h in split])
    r.acc[...] = jnp.dot(r.matrix[own_slot], r.tables[...], preferred_element_type=f32)

    def gather(p):
        top, deep, h = pieces[p]
        rows = slice(top, top + deep)
        cut = slice(h * LANES, (h + 1) * LANES)
        for o in range(1, d.big_z):
            src = lax.rem(z + o, d.big_z)
            below = (src < z) & (lax.rem(src, 2) == 1)
            above = (src > z) & (lax.rem(src, 2) == 0)

            @pl.when((src == partner) | below | above)
            def _(src=src):
                arrival(src, p).wait_recv()
                r.acc[rows, cut] += r.z_recv[src, rows, cut].astype(f32)

    early = [piece_of[q, split[0]] for q in range(d.blocks - 1)] if len(split) > 1 else []
    for p in list(range(whole)) + early:
        relays(p)
    for p in range(whole):
        gather(p)
    loads[2].wait()
    half = d.big_y * d.step

    def c_copy(q, j):
        return remote(r.c_send.at[q, j], r.c_recv.at[q, j], r.c_ss.at[q, j], r.c_rs.at[q, j], c_peer)

    def y_copy(q, j, o):
        return remote(
            r.y_send.at[q, j, o], r.y_recv.at[q, j, o], r.y_ss.at[q, j, o], r.y_rs.at[q, j, o], y_peers[o]
        )

    def project(q):
        rows = slice(q * block, (q + 1) * block)
        counted = r.local[own_slot, rows, d.fan_one : d.fan_one + 1].astype(f32)
        r.means[rows, :] = (r.acc[rows, :] / counted).astype(bf16)

        def tile(j, carry):
            cut = pl.ds(pl.multiple_of(j * d.tile, LANES), d.tile)
            r.tot[...] = r.part[j, rows, :] + jnp.dot(
                r.means[rows, :], r.w_pool[:, cut], preferred_element_type=f32
            )
            far = pl.ds(pl.multiple_of(other * half, half), half)
            near = pl.ds(pl.multiple_of(core * half, half), half)
            r.c_send[q, j] = r.tot[far, :].astype(bf16)
            c_copy(q, j).start()
            r.mine[q, j] = r.tot[near, :].reshape(d.big_y, d.step, d.tile)
            return carry

        lax.fori_loop(0, TILES, tile, 0)

    def across(q):
        def tile(j, carry):
            c_copy(q, j).wait()
            r.mine[q, j] += r.c_recv[q, j].astype(f32).reshape(d.big_y, d.step, d.tile)
            for o in range(d.big_y - 1):
                r.y_send[q, j, o] = r.mine[q, j, lax.rem(y + 1 + o, d.big_y)].astype(bf16)
                y_copy(q, j, o).start()
            return carry

        lax.fori_loop(0, TILES, tile, 0)

    def p_copy(q, o):
        at = r.proj.at[pl.ds(pl.multiple_of(q * block + place * d.step, d.step), d.step)]
        return remote(at, at, r.p_ss.at[q, o], r.p_rs.at[q, o], f_peers[o])

    def finish(q):
        mine = slice(q * d.step, (q + 1) * d.step)
        for j in range(TILES):
            total = r.mine[q, j, y]
            for o in range(d.big_y - 1):
                y_copy(q, j, o).wait()
                total = total + r.y_recv[q, j, o].astype(f32)
            r.hidden[mine, j * d.tile : (j + 1) * d.tile] = jnp.maximum(total, 0.0)
        value = jnp.dot(r.hidden[mine, :].astype(bf16), r.v_pool[...], preferred_element_type=f32)
        at = pl.ds(pl.multiple_of(q * block + place * d.step, d.step), d.step)
        r.proj[at, :] = value.astype(bf16).astype(r.proj.dtype)
        for o in range(d.feats - 1):
            p_copy(q, o).start()

    for q in range(d.blocks):
        for h in split:
            if piece_of[q, h] not in early:
                relays(piece_of[q, h])
        if q > 0:
            across(q - 1)
        for h in split:
            gather(piece_of[q, h])
        project(q)
        if q == 0:
            loads[3].wait()
            loads[4].wait()
            for o in range(d.feats - 1):
                for copy in v_copies(o):
                    copy.wait()
        if q > 0:
            finish(q - 1)
    across(d.blocks - 1)
    finish(d.blocks - 1)
    own_two = jnp.dot(r.hidden[d.step :, :].astype(bf16), r.v_self[...], preferred_element_type=f32)
    for q in range(d.blocks):
        for o in range(d.feats - 1):
            p_copy(q, o).wait()
    r.mixed[...] = (
        jnp.dot(r.matrix_two[...], r.proj[...].astype(bf16), preferred_element_type=f32) * r.scale_two[...]
    )

    def m_copy(o):
        return remote(r.m_send.at[o], r.m_recv.at[o], r.m_ss.at[o], r.m_rs.at[o], n_peers[o])

    ways = sorted(range(d.shards - 1), key=lambda o: abs(o + 1 - d.shards // 2))
    for o in ways:
        to = pl.multiple_of(lax.rem(node + 1 + o, d.shards) * d.piece, 16)
        r.m_send[o] = r.mixed[pl.ds(to, d.piece), :].astype(bf16)
        m_copy(o).start()
    total = own_two + r.mixed[pl.ds(pl.multiple_of(node * d.piece, 16), d.piece), :]
    for s in range(d.big_z - 1):
        for p in range(len(pieces)):
            final_copy(s, p).wait_send()
    for o in reversed(ways):
        m_copy(o).wait()
        total = total + r.m_recv[o].astype(f32)
    scale = lax.rsqrt(jnp.mean(total * total, axis=1, keepdims=True) + 1e-06)
    r.out[...] = (total * scale).astype(bf16)


def body(
    feature_table,
    hub_table,
    first_self,
    first_pooled,
    second_self,
    second_pooled,
    first_lists,
    first_counts,
    second_lists,
    second_counts,
):
    d = types.SimpleNamespace()
    d.shards = lax.axis_size("node")
    d.feats = lax.axis_size("feat")
    d.big_x = 2 ** ((d.shards.bit_length() - 1) // 2)
    d.big_z = d.shards // d.big_x
    d.big_y = d.feats // CORES
    d.rows, d.width = feature_table.shape
    d.hubs_here = hub_table.shape[0]
    d.front, d.fan_one = first_lists.shape
    d.targets, d.fan_two = second_lists.shape
    d.piece = d.targets // d.feats
    d.out_width = second_self.shape[1]
    d.hidden_part = second_self.shape[0]
    units = d.hidden_part * d.feats
    d.tile = units // TILES
    d.depth = d.big_x * d.rows + -(-d.big_x * HUB_ROWS // LANES) * LANES
    d.chunks = d.width // LANES
    d.step = (d.front - d.targets) // d.feats
    d.blocks = d.front // (d.step * d.feats)
    assert d.step * d.feats * d.blocks == d.front and d.piece % d.step == 0
    order = []
    for q in range(d.blocks):
        for c in range(CORES):
            for yy in range(d.big_y):
                f = yy * CORES + c
                start = d.targets + f * d.step if q == 0 else f * d.piece + (q - 1) * d.step
                order.append((q * d.step * d.feats + (c * d.big_y + yy) * d.step, start, f))
    d.order = order
    bf16, f32, i32, i16 = jnp.bfloat16, jnp.float32, jnp.int32, jnp.int16
    dma, vm = pltpu.SemaphoreType.DMA, pltpu.VMEM
    zs, xs, ys, ns, fs = d.big_z - 1, d.big_x - 1, d.big_y - 1, d.shards - 1, d.feats - 1
    count = d.chunks * d.blocks
    half = d.big_y * d.step
    kind = bf16 if d.step % 16 == 0 else f32
    scratch = dict(
        tables=vm((d.depth, d.width), bf16),
        w_self=vm((d.width, units), bf16),
        w_pool=vm((d.width, units), bf16),
        v_self=vm((units, d.out_width), bf16),
        v_pool=vm((units, d.out_width), bf16),
        hubs=vm((HUB_ROWS, d.width), bf16),
        raw=vm((LIST_ROWS, d.front), i32),
        raw_two=vm((8, d.targets), i32),
        l_send=vm((zs, LIST_ROWS, d.front), i16),
        l_recv=vm((d.big_z, LIST_ROWS, d.front), i16),
        s_send=vm((8, d.targets), i32),
        s_recv=vm((d.shards, 8, d.targets), i32),
        turned=vm((d.targets, 8), i32),
        local=vm((d.big_z, d.front, LIST_ROWS), i32),
        matrix=vm((d.big_z, d.front, d.depth), bf16),
        matrix_two=vm((d.shards * d.piece, d.front), bf16),
        scale_two=vm((d.shards * d.piece, 1), f32),
        part=vm((TILES, d.front, d.tile), f32),
        hold=vm((zs, d.front, d.width), f32),
        z_send=vm((zs, d.front, d.width), bf16),
        z_recv=vm((2 * d.big_z, d.front, d.width), bf16),
        acc=vm((d.front, d.width), f32),
        means=vm((d.front, d.width), bf16),
        tot=vm((d.step * d.feats, d.tile), f32),
        mine=vm((d.blocks, TILES, d.big_y, d.step, d.tile), f32),
        c_send=vm((d.blocks, TILES, half, d.tile), bf16),
        c_recv=vm((d.blocks, TILES, half, d.tile), bf16),
        y_send=vm((d.blocks, TILES, ys, d.step, d.tile), bf16),
        y_recv=vm((d.blocks, TILES, ys, d.step, d.tile), bf16),
        hidden=vm((d.blocks * d.step, units), f32),
        proj=vm((d.front, d.out_width), kind),
        mixed=vm((d.shards * d.piece, d.out_width), f32),
        m_send=vm((ns, d.piece, d.out_width), bf16),
        m_recv=vm((ns, d.piece, d.out_width), bf16),
        load=dma((5,)),
        x_ss=dma((d.chunks, xs)),
        x_rs=dma((d.chunks, xs)),
        h_ss=dma((xs,)),
        h_rs=dma((xs,)),
        l_ss=dma((zs,)),
        l_rs=dma((zs,)),
        s_ss=dma((ns,)),
        s_rs=dma((ns,)),
        v_ss=dma((2, fs)),
        v_rs=dma((2, fs)),
        z_ss=dma((zs, count)),
        z_rs=dma((2 * d.big_z, count)),
        c_ss=dma((d.blocks, TILES)),
        c_rs=dma((d.blocks, TILES)),
        y_ss=dma((d.blocks, TILES, ys)),
        y_rs=dma((d.blocks, TILES, ys)),
        p_ss=dma((d.blocks, fs)),
        p_rs=dma((d.blocks, fs)),
        m_ss=dma((ns,)),
        m_rs=dma((ns,)),
    )
    inputs = ["table", "hub", "self_one", "pool_one", "self_two", "pool_two"]
    inputs += ["lists_one", "counts_one", "lists_two", "counts_two"]
    names = inputs + ["out"] + list(scratch)
    vmem = pl.BlockSpec(memory_space=pltpu.VMEM)
    hbm = pl.BlockSpec(memory_space=pl.ANY)
    return pl.pallas_call(
        functools.partial(main_kernel, d, names),
        out_shape=jax.ShapeDtypeStruct((d.piece, d.out_width), bf16),
        in_specs=[hbm, vmem, hbm, hbm, hbm, hbm, vmem, vmem, vmem, vmem],
        out_specs=vmem,
        scratch_shapes=list(scratch.values()),
        compiler_params=pltpu.CompilerParams(
            collective_id=1, has_side_effects=True, vmem_limit_bytes=60 * 1024 * 1024
        ),
    )(
        feature_table,
        hub_table,
        first_self,
        first_pooled,
        second_self,
        second_pooled,
        first_lists.T,
        first_counts[None, :],
        second_lists.T,
        second_counts[None, :],
    )


def solution(mesh):
    return jax.shard_map(
        body,
        mesh=mesh,
        in_specs=(
            P("node", "feat"),
            P("node", "feat"),
            P("feat", None),
            P("feat", None),
            P("feat", None),
            P("feat", None),
            P("node", None),
            P("node"),
            P("node", None),
            P("node"),
        ),
        out_specs=P(("node", "feat"), None),
        check_vma=False,
    )
```

```python
import functools
import types

import jax
import jax.numpy as jnp
from jax import lax
from jax.experimental import pallas as pl
from jax.experimental.pallas import tpu as pltpu
from jax.sharding import PartitionSpec as P

MESH = pl.DeviceIdType.MESH
CORES = 2
LANES = 128
TILES = 4
HUB_ROWS = 16
LIST_ROWS = 16


def greet(peers):
    barrier = pltpu.get_barrier_semaphore()
    for peer in peers:
        pl.semaphore_signal(barrier, inc=1, device_id=peer, device_id_type=MESH)
    pl.semaphore_wait(barrier, len(peers))


def remote(src, dst, sends, recvs, peer):
    return pltpu.make_async_remote_copy(
        src_ref=src, dst_ref=dst, send_sem=sends, recv_sem=recvs, device_id=peer, device_id_type=MESH
    )


def count_tiles(local, fan, names, store):
    rows = local.shape[0]
    local = local.astype(jnp.int16)
    one, zero = jnp.bfloat16(1), jnp.bfloat16(0)
    picked = [jnp.broadcast_to(local[:, k : k + 1], (rows, LANES)) for k in range(fan)]
    for at, columns in enumerate(names):
        columns = columns(rows)
        total = jnp.zeros((rows, LANES), jnp.bfloat16)
        for k in range(fan):
            total = total + jnp.where(picked[k] == columns, one, zero)
        store(at * LANES, total)


def plain_names(base, count):
    def name(start, rows):
        return (lax.broadcasted_iota(jnp.int32, (rows, LANES), 1) + start).astype(jnp.int16)

    return [functools.partial(name, base + at * LANES) for at in range(count)]


def main_kernel(d, names, *refs):
    r = types.SimpleNamespace(**dict(zip(names, refs)))
    f32, bf16 = jnp.float32, jnp.bfloat16
    node, feat = lax.axis_index("node"), lax.axis_index("feat")
    z, x = node // d.big_x, lax.rem(node, d.big_x)
    y, core = feat // CORES, lax.rem(feat, CORES)
    other = 1 - core
    place = core * d.big_y + y
    x_peers = [{"node": z * d.big_x + lax.rem(x + o, d.big_x)} for o in range(1, d.big_x)]
    y_peers = [{"feat": lax.rem(y + o, d.big_y) * CORES + core} for o in range(1, d.big_y)]
    n_peers = [{"node": lax.rem(node + o, d.shards)} for o in range(1, d.shards)]
    f_peers = [{"feat": lax.rem(feat + o, d.feats)} for o in range(1, d.feats)]
    c_peer = {"feat": y * CORES + other}

    def z_peer(to):
        return {"node": to * d.big_x + x}

    my_rows = pl.ds(pl.multiple_of(x * d.rows, d.rows), d.rows)
    my_units = pl.ds(pl.multiple_of(feat * d.hidden_part, d.hidden_part), d.hidden_part)
    loads = [
        pltpu.make_async_copy(r.table, r.tables.at[my_rows], r.load.at[0]),
        pltpu.make_async_copy(r.self_one, r.w_self, r.load.at[1]),
        pltpu.make_async_copy(r.pool_one, r.w_pool, r.load.at[2]),
        pltpu.make_async_copy(r.self_two, r.v_self.at[my_units], r.load.at[3]),
        pltpu.make_async_copy(r.pool_two, r.v_pool.at[my_units], r.load.at[4]),
    ]
    for copy in loads:
        copy.start()
    hub_top = d.big_x * d.rows
    r.hubs[...] = jnp.zeros(r.hubs.shape, bf16)
    r.hubs[0 : d.hubs_here, :] = r.hub[...]
    r.tables[hub_top : d.depth, :] = jnp.zeros((d.depth - hub_top, d.width), bf16)
    my_hubs = pl.ds(pl.multiple_of(hub_top + x * HUB_ROWS, HUB_ROWS), HUB_ROWS)
    r.tables[my_hubs, :] = r.hubs[...]
    greet(n_peers + f_peers)

    def x_copy(h, o):
        cut = pl.ds(h * LANES, LANES)
        return remote(
            r.table.at[:, cut], r.tables.at[my_rows, cut], r.x_ss.at[h, o], r.x_rs.at[h, o], x_peers[o]
        )


    def h_copy(o):
        return remote(r.hubs, r.tables.at[my_hubs], r.h_ss.at[o], r.h_rs.at[o], x_peers[o])

    for o in range(d.big_x - 1):
        h_copy(o).start()
        x_copy(0, o).start()

    line = lax.broadcasted_iota(jnp.int32, (LIST_ROWS, d.front), 0)
    r.raw[...] = jnp.full((LIST_ROWS, d.front), -1, jnp.int32)
    r.raw[0 : d.fan_one, :] = r.lists_one[...]
    counts = jnp.broadcast_to(r.counts_one[...].reshape(1, d.front), (LIST_ROWS, d.front))
    entry = jnp.where(line < jnp.minimum(counts, d.fan_one), r.raw[...], -1)

    def decode(to):
        here = entry - to * (d.big_x * d.rows)
        found = jnp.where((here >= 0) & (here < hub_top), here, -1)
        for slot in range(d.big_x):
            hub = entry - (d.shards * d.rows + (to * d.big_x + slot) * d.hubs_here)
            found = jnp.where(
                (hub >= 0) & (hub < d.hubs_here), hub + (hub_top + slot * HUB_ROWS), found
            )
        return found

    def l_copy(o):
        to = lax.rem(z + o, d.big_z)
        return remote(
            r.l_send.at[o - 1], r.l_recv.at[z], r.l_ss.at[o - 1], r.l_rs.at[o - 1], z_peer(to)
        )

    for o in range(1, d.big_z):
        r.l_send[o - 1] = decode(lax.rem(z + o, d.big_z)).astype(jnp.int16)
        l_copy(o).start()

    def place_rows(slot, found):
        turned = found.T
        for to, start, _ in d.order:
            r.local[slot, to : to + d.step, :] = turned[start : start + d.step, :]

    own_slot = d.big_z - 1
    place_rows(own_slot, jnp.where(line == d.fan_one, counts, decode(z)))

    line_two = lax.broadcasted_iota(jnp.int32, (8, d.targets), 0)
    counts_two = jnp.broadcast_to(r.counts_two[...], (8, d.targets))
    r.raw_two[...] = jnp.full((8, d.targets), -1, jnp.int32)
    r.raw_two[0 : d.fan_two, :] = r.lists_two[...]
    second = jnp.where(line_two < jnp.minimum(counts_two, d.fan_two), r.raw_two[...], -1)
    second = jnp.where(line_two == d.fan_two, counts_two, second)
    r.s_send[...] = second
    r.s_recv[node] = second

    def s_copy(o):
        return remote(r.s_send, r.s_recv.at[node], r.s_ss.at[o], r.s_rs.at[o], n_peers[o])

    for o in range(d.shards - 1):
        s_copy(o).start()

    for h in range(1, d.chunks):
        for o in range(d.big_x - 1):
            x_copy(h, o).start()

    def v_copies(o):
        return [
            remote(r.self_two, r.v_self.at[my_units], r.v_ss.at[0, o], r.v_rs.at[0, o], f_peers[o]),
            remote(r.pool_two, r.v_pool.at[my_units], r.v_ss.at[1, o], r.v_rs.at[1, o], f_peers[o]),
        ]

    for o in range(d.feats - 1):
        for copy in v_copies(o):
            copy.start()

    own_rows = pl.ds(pl.multiple_of(x * d.rows, d.rows), d.front)

    def own_part(j, carry):
        cut = pl.ds(pl.multiple_of(j * d.tile, LANES), d.tile)
        value = jnp.dot(r.tables[own_rows, :], r.w_self[:, cut], preferred_element_type=f32)
        for to, start, _ in d.order:
            r.part[j, to : to + d.step, :] = value[start : start + d.step, :]
        return carry

    turn = 2 * z // d.big_z

    turns = max(d.big_z - 1, 1)

    def target_of(s):
        mirrored = z + turn * (d.big_z - 1 - 2 * z)
        back = (s + mirrored) // turns
        to = (1 - back) * (d.big_z - 1 - s) + back * (s + mirrored - turns)
        return to + turn * (d.big_z - 1 - 2 * to)

    for o in range(1, d.big_z):
        l_copy(o).wait()

    def take_list(s, carry):
        place_rows(s, r.l_recv[target_of(s)].astype(jnp.int32))
        return carry

    lax.fori_loop(0, d.big_z - 1, take_list, 0)

    tile_names = plain_names(0, d.depth // LANES)

    def fill(slot):
        def group(i, carry):
            row0 = pl.multiple_of(i * 32, 32)

            def store(start, value):
                r.matrix[slot, pl.ds(row0, 32), start : start + LANES] = value

            count_tiles(r.local[slot, pl.ds(row0, 32), :], d.fan_one, tile_names, store)
            return carry

        lax.fori_loop(0, d.front // 32, group, 0)

    last = d.chunks - 1
    block = d.feats * d.step
    split = [h for h in (last - 1, last) if h > 0 or h == last]
    pieces = [(0, d.front, h) for h in range(split[0])]
    whole = len(pieces)
    piece_of = {}
    for group in (range(d.blocks - 1), (d.blocks - 1,)):
        for h in split:
            for q in group:
                piece_of[q, h] = len(pieces)
                pieces.append((q * block, block, h))
    odd = lax.rem(z, 2)
    partner = z + 1 - 2 * odd

    def region(p):
        top, deep, h = pieces[p]
        return pl.ds(top, deep), pl.ds(h * LANES, LANES)

    def held(s):
        to = target_of(s)
        return ((odd == 1) & (to > z)) | ((odd == 0) & (to < z))

    def led(s):
        to = target_of(s)
        return ((odd == 0) & (to > z + 1)) | ((odd == 1) & (to < z - 1))

    def hop_copy(s, p, slot, peer):
        rows, cut = region(p)
        return remote(
            r.z_send.at[s, rows, cut],
            r.z_recv.at[slot, rows, cut],
            r.z_ss.at[s, p],
            r.z_rs.at[slot, p],
            z_peer(peer),
        )

    def led_copy(s, p):
        return hop_copy(s, p, d.big_z + target_of(s), partner)

    def final_copy(s, p):
        return hop_copy(s, p, z, target_of(s))

    def arrival(slot, p):
        rows, cut = region(p)
        at = r.z_recv.at[slot, rows, cut]
        return remote(at, at, r.z_rs.at[slot, p], r.z_rs.at[slot, p], z_peer(lax.rem(z + 1, d.big_z)))

    def relay(p):
        top, deep, h = pieces[p]
        rows = slice(top, top + deep)
        cut = slice(h * LANES, (h + 1) * LANES)

        def one(s, carry):
            @pl.when(held(s))
            def _():
                slot = d.big_z + target_of(s)
                arrival(slot, p).wait_recv()
                r.z_send[s, rows, cut] = (
                    r.hold[s, rows, cut] + r.z_recv[slot, rows, cut].astype(f32)
                ).astype(bf16)
                final_copy(s, p).start()

            return carry

        lax.fori_loop(0, d.big_z - 1, one, 0)

    def sums(h, s):
        cut = slice(h * LANES, (h + 1) * LANES)
        value = jnp.dot(r.matrix[s], r.tables[:, cut], preferred_element_type=f32)

        kept = held(s)

        @pl.when(kept)
        def _():
            r.hold[s, :, cut] = value

        @pl.when(jnp.logical_not(kept))
        def _():
            r.z_send[s, :, cut] = value.astype(bf16)

    def launch(s, p):
        @pl.when(led(s))
        def _():
            led_copy(s, p).start()

        @pl.when(jnp.logical_not(held(s) | led(s)))
        def _():
            final_copy(s, p).start()

    def send_all(ps):
        for p in ps:
            for s in range(d.big_z - 1):
                launch(s, p)

    def chunk(h):
        for o in range(d.big_x - 1):
            x_copy(h, o).wait()

        def one_target(s, carry):
            sums(h, s)
            if h < split[0]:
                launch(s, h)
            return carry

        lax.fori_loop(0, d.big_z - 1, one_target, 0)

    relayed = set()

    def relays(p):
        if d.big_z > 2 and p not in relayed:
            relayed.add(p)

            relay(p)

    def fill_second(n, carry):
        local = (r.s_recv[n]).T
        r.turned[...] = local
        mine = r.turned[pl.ds(pl.multiple_of(feat * d.piece, 8), d.piece), :]
        row = pl.multiple_of(n * d.piece, 16)

        def store(start, value):
            r.matrix_two[pl.ds(row, d.piece), start : start + LANES] = value

        found = jnp.clip(mine[:, 0 : d.fan_two] - node * d.front, -1, d.front)
        count_tiles(found, d.fan_two, second_names, store)
        r.scale_two[pl.ds(row, d.piece), :] = 1.0 / mine[:, d.fan_two : d.fan_two + 1].astype(f32)
        return carry

    def second_name(start, rows):
        lane = lax.broadcasted_iota(jnp.int32, (rows, LANES), 1) + start
        q = lane // block
        rest = lane - q * block
        spot = rest // d.step
        within = rest - spot * d.step
        c = spot // d.big_y
        f = (spot - c * d.big_y) * CORES + c
        early = d.targets + f * d.step + within
        late = f * d.piece + (q - 1) * d.step + within
        return jnp.where(q == 0, early, late).astype(jnp.int16)

    second_names = [functools.partial(second_name, at) for at in range(0, d.front, LANES)]

    fill(0)
    if d.big_z > 2:
        fill(1)
    for o in range(d.big_x - 1):
        x_copy(0, o).wait()
        h_copy(o).wait()
    loads[0].wait()

    def first_sums(s, carry):
        @pl.when(s > 1)
        def _():
            fill(s)

        sums(0, s)
        if split[0] > 0:
            launch(s, 0)
        return carry

    lax.fori_loop(0, d.big_z - 1, first_sums, 0)
    loads[1].wait()
    lax.fori_loop(0, TILES, own_part, 0)
    for h in range(1, d.chunks):
        if h < last - 1:
            relays(h - 1)
        chunk(h)
        if h == last - 1:
            if h > 0:
                send_all([piece_of[q, h] for q in range(d.blocks - 1)])
            if h - 1 >= 0 and split[0] > h - 1:
                relays(h - 1)
        if h == max(last - 2, 1):
            for o in range(d.shards - 1):
                s_copy(o).wait()
            lax.fori_loop(0, d.shards, fill_second, 0)
        if h == last - 1:
            fill(own_slot)
    if last <= 1:
        if last == 0:
            for o in range(d.shards - 1):
                s_copy(o).wait()
            lax.fori_loop(0, d.shards, fill_second, 0)
        fill(own_slot)
        send_all(range(whole, len(pieces)))
    else:
        send_all([piece_of[q, last] for q in range(d.blocks - 1)])
        send_all([piece_of[d.blocks - 1, h] for h in split])
    r.acc[...] = jnp.dot(r.matrix[own_slot], r.tables[...], preferred_element_type=f32)

    def gather(p):
        top, deep, h = pieces[p]
        rows = slice(top, top + deep)
        cut = slice(h * LANES, (h + 1) * LANES)
        for o in range(1, d.big_z):
            src = lax.rem(z + o, d.big_z)
            below = (src < z) & (lax.rem(src, 2) == 1)
            above = (src > z) & (lax.rem(src, 2) == 0)

            @pl.when((src == partner) | below | above)
            def _(src=src):
                arrival(src, p).wait_recv()
                r.acc[rows, cut] += r.z_recv[src, rows, cut].astype(f32)

    rest = [piece_of[d.blocks - 1, h] for h in split]
    for p in range(len(pieces)):
        if p not in rest:
            relays(p)
    for p in range(whole):
        gather(p)
    loads[2].wait()
    half = d.big_y * d.step

    def c_copy(q, j):
        return remote(r.c_send.at[q, j], r.c_recv.at[q, j], r.c_ss.at[q, j], r.c_rs.at[q, j], c_peer)

    def y_copy(q, j, o):
        return remote(
            r.y_send.at[q, j, o], r.y_recv.at[q, j, o], r.y_ss.at[q, j, o], r.y_rs.at[q, j, o], y_peers[o]
        )

    def project(q):
        rows = slice(q * block, (q + 1) * block)
        counted = r.local[own_slot, rows, d.fan_one : d.fan_one + 1].astype(f32)
        r.means[rows, :] = (r.acc[rows, :] / counted).astype(bf16)

        def tile(j, carry):
            cut = pl.ds(pl.multiple_of(j * d.tile, LANES), d.tile)
            r.tot[...] = r.part[j, rows, :] + jnp.dot(
                r.means[rows, :], r.w_pool[:, cut], preferred_element_type=f32
            )
            far = pl.ds(pl.multiple_of(other * half, half), half)
            near = pl.ds(pl.multiple_of(core * half, half), half)
            r.c_send[q, j] = r.tot[far, :].astype(bf16)
            c_copy(q, j).start()
            r.mine[q, j] = r.tot[near, :].reshape(d.big_y, d.step, d.tile)
            return carry

        lax.fori_loop(0, TILES, tile, 0)

    def across(q):
        def tile(j, carry):
            c_copy(q, j).wait()
            r.mine[q, j] += r.c_recv[q, j].astype(f32).reshape(d.big_y, d.step, d.tile)
            for o in range(d.big_y - 1):
                r.y_send[q, j, o] = r.mine[q, j, lax.rem(y + 1 + o, d.big_y)].astype(bf16)
                y_copy(q, j, o).start()
            return carry

        lax.fori_loop(0, TILES, tile, 0)

    def p_copy(q, o):
        at = r.proj.at[pl.ds(pl.multiple_of(q * block + place * d.step, d.step), d.step)]
        return remote(at, at, r.p_ss.at[q, o], r.p_rs.at[q, o], f_peers[o])

    def finish(q):
        mine = slice(q * d.step, (q + 1) * d.step)
        for j in range(TILES):
            total = r.mine[q, j, y]
            for o in range(d.big_y - 1):
                y_copy(q, j, o).wait()
                total = total + r.y_recv[q, j, o].astype(f32)
            r.hidden[mine, j * d.tile : (j + 1) * d.tile] = jnp.maximum(total, 0.0)
        value = jnp.dot(r.hidden[mine, :].astype(bf16), r.v_pool[...], preferred_element_type=f32)
        at = pl.ds(pl.multiple_of(q * block + place * d.step, d.step), d.step)
        r.proj[at, :] = value.astype(bf16).astype(r.proj.dtype)
        for o in range(d.feats - 1):
            p_copy(q, o).start()

    for q in range(d.blocks):
        if q == d.blocks - 2:
            relays(rest[0])
        if q == d.blocks - 1:
            for p in rest:
                relays(p)
        if q > 0:
            across(q - 1)
        for h in split:
            gather(piece_of[q, h])
        project(q)
        if q == 0:
            loads[3].wait()
            loads[4].wait()
            for o in range(d.feats - 1):
                for copy in v_copies(o):
                    copy.wait()
    for q in range(d.blocks - 2):
        finish(q)
    across(d.blocks - 1)
    for q in range(max(d.blocks - 2, 0), d.blocks):
        finish(q)
    own_two = jnp.dot(r.hidden[d.step :, :].astype(bf16), r.v_self[...], preferred_element_type=f32)
    for q in range(d.blocks):
        for o in range(d.feats - 1):
            p_copy(q, o).wait()
    r.mixed[...] = (
        jnp.dot(r.matrix_two[...], r.proj[...].astype(bf16), preferred_element_type=f32) * r.scale_two[...]
    )

    def m_copy(o):
        return remote(r.m_send.at[o], r.m_recv.at[o], r.m_ss.at[o], r.m_rs.at[o], n_peers[o])

    ways = sorted(range(d.shards - 1), key=lambda o: abs(o + 1 - d.shards // 2))
    for o in ways:
        to = pl.multiple_of(lax.rem(node + 1 + o, d.shards) * d.piece, 16)
        r.m_send[o] = r.mixed[pl.ds(to, d.piece), :].astype(bf16)
        m_copy(o).start()
    total = own_two + r.mixed[pl.ds(pl.multiple_of(node * d.piece, 16), d.piece), :]
    for s in range(d.big_z - 1):
        for p in range(len(pieces)):
            final_copy(s, p).wait_send()
    for o in reversed(ways):
        m_copy(o).wait()
        total = total + r.m_recv[o].astype(f32)
    scale = lax.rsqrt(jnp.mean(total * total, axis=1, keepdims=True) + 1e-06)
    r.out[...] = (total * scale).astype(bf16)


def body(
    feature_table,
    hub_table,
    first_self,
    first_pooled,
    second_self,
    second_pooled,
    first_lists,
    first_counts,
    second_lists,
    second_counts,
):
    d = types.SimpleNamespace()
    d.shards = lax.axis_size("node")
    d.feats = lax.axis_size("feat")
    d.big_x = 2 ** ((d.shards.bit_length() - 1) // 2)
    d.big_z = d.shards // d.big_x
    d.big_y = d.feats // CORES
    d.rows, d.width = feature_table.shape
    d.hubs_here = hub_table.shape[0]
    d.front, d.fan_one = first_lists.shape
    d.targets, d.fan_two = second_lists.shape
    d.piece = d.targets // d.feats
    d.out_width = second_self.shape[1]
    d.hidden_part = second_self.shape[0]
    units = d.hidden_part * d.feats
    d.tile = units // TILES
    d.depth = d.big_x * d.rows + -(-d.big_x * HUB_ROWS // LANES) * LANES
    d.chunks = d.width // LANES
    d.step = (d.front - d.targets) // d.feats
    d.blocks = d.front // (d.step * d.feats)
    assert d.step * d.feats * d.blocks == d.front and d.piece % d.step == 0
    order = []
    for q in range(d.blocks):
        for c in range(CORES):
            for yy in range(d.big_y):
                f = yy * CORES + c
                start = d.targets + f * d.step if q == 0 else f * d.piece + (q - 1) * d.step
                order.append((q * d.step * d.feats + (c * d.big_y + yy) * d.step, start, f))
    d.order = order
    bf16, f32, i32, i16 = jnp.bfloat16, jnp.float32, jnp.int32, jnp.int16
    dma, vm = pltpu.SemaphoreType.DMA, pltpu.VMEM
    zs, xs, ys, ns, fs = d.big_z - 1, d.big_x - 1, d.big_y - 1, d.shards - 1, d.feats - 1
    count = d.chunks * d.blocks
    half = d.big_y * d.step
    kind = bf16 if d.step % 16 == 0 else f32
    scratch = dict(
        tables=vm((d.depth, d.width), bf16),
        w_self=vm((d.width, units), bf16),
        w_pool=vm((d.width, units), bf16),
        v_self=vm((units, d.out_width), bf16),
        v_pool=vm((units, d.out_width), bf16),
        hubs=vm((HUB_ROWS, d.width), bf16),
        raw=vm((LIST_ROWS, d.front), i32),
        raw_two=vm((8, d.targets), i32),
        l_send=vm((zs, LIST_ROWS, d.front), i16),
        l_recv=vm((d.big_z, LIST_ROWS, d.front), i16),
        s_send=vm((8, d.targets), i32),
        s_recv=vm((d.shards, 8, d.targets), i32),
        turned=vm((d.targets, 8), i32),
        local=vm((d.big_z, d.front, LIST_ROWS), i32),
        matrix=vm((d.big_z, d.front, d.depth), bf16),
        matrix_two=vm((d.shards * d.piece, d.front), bf16),
        scale_two=vm((d.shards * d.piece, 1), f32),
        part=vm((TILES, d.front, d.tile), f32),
        hold=vm((zs, d.front, d.width), f32),
        z_send=vm((zs, d.front, d.width), bf16),
        z_recv=vm((2 * d.big_z, d.front, d.width), bf16),
        acc=vm((d.front, d.width), f32),
        means=vm((d.front, d.width), bf16),
        tot=vm((d.step * d.feats, d.tile), f32),
        mine=vm((d.blocks, TILES, d.big_y, d.step, d.tile), f32),
        c_send=vm((d.blocks, TILES, half, d.tile), bf16),
        c_recv=vm((d.blocks, TILES, half, d.tile), bf16),
        y_send=vm((d.blocks, TILES, ys, d.step, d.tile), bf16),
        y_recv=vm((d.blocks, TILES, ys, d.step, d.tile), bf16),
        hidden=vm((d.blocks * d.step, units), f32),
        proj=vm((d.front, d.out_width), kind),
        mixed=vm((d.shards * d.piece, d.out_width), f32),
        m_send=vm((ns, d.piece, d.out_width), bf16),
        m_recv=vm((ns, d.piece, d.out_width), bf16),
        load=dma((5,)),
        x_ss=dma((d.chunks, xs)),
        x_rs=dma((d.chunks, xs)),
        h_ss=dma((xs,)),
        h_rs=dma((xs,)),
        l_ss=dma((zs,)),
        l_rs=dma((zs,)),
        s_ss=dma((ns,)),
        s_rs=dma((ns,)),
        v_ss=dma((2, fs)),
        v_rs=dma((2, fs)),
        z_ss=dma((zs, count)),
        z_rs=dma((2 * d.big_z, count)),
        c_ss=dma((d.blocks, TILES)),
        c_rs=dma((d.blocks, TILES)),
        y_ss=dma((d.blocks, TILES, ys)),
        y_rs=dma((d.blocks, TILES, ys)),
        p_ss=dma((d.blocks, fs)),
        p_rs=dma((d.blocks, fs)),
        m_ss=dma((ns,)),
        m_rs=dma((ns,)),
    )
    inputs = ["table", "hub", "self_one", "pool_one", "self_two", "pool_two"]
    inputs += ["lists_one", "counts_one", "lists_two", "counts_two"]
    names = inputs + ["out"] + list(scratch)
    vmem = pl.BlockSpec(memory_space=pltpu.VMEM)
    hbm = pl.BlockSpec(memory_space=pl.ANY)
    return pl.pallas_call(
        functools.partial(main_kernel, d, names),
        out_shape=jax.ShapeDtypeStruct((d.piece, d.out_width), bf16),
        in_specs=[hbm, vmem, hbm, hbm, hbm, hbm, vmem, vmem, vmem, vmem],
        out_specs=vmem,
        scratch_shapes=list(scratch.values()),
        compiler_params=pltpu.CompilerParams(
            collective_id=1, has_side_effects=True, vmem_limit_bytes=60 * 1024 * 1024
        ),
    )(
        feature_table,
        hub_table,
        first_self,
        first_pooled,
        second_self,
        second_pooled,
        first_lists.T,
        first_counts,
        second_lists.T,
        second_counts[None, :],
    )


def solution(mesh):
    return jax.shard_map(
        body,
        mesh=mesh,
        in_specs=(
            P("node", "feat"),
            P("node", "feat"),
            P("feat", None),
            P("feat", None),
            P("feat", None),
            P("feat", None),
            P("node", None),
            P("node"),
            P("node", None),
            P("node"),
        ),
        out_specs=P(("node", "feat"), None),
        check_vma=False,
    )
```

```python
import functools
import types

import jax
import jax.numpy as jnp
from jax import lax
from jax.experimental import pallas as pl
from jax.experimental.pallas import tpu as pltpu
from jax.sharding import PartitionSpec as P

MESH = pl.DeviceIdType.MESH
CORES = 2
LANES = 128
TILES = 4
HUB_ROWS = 16
LIST_ROWS = 16


def greet(peers):
    barrier = pltpu.get_barrier_semaphore()
    for peer in peers:
        pl.semaphore_signal(barrier, inc=1, device_id=peer, device_id_type=MESH)
    pl.semaphore_wait(barrier, len(peers))


def remote(src, dst, sends, recvs, peer):
    return pltpu.make_async_remote_copy(
        src_ref=src, dst_ref=dst, send_sem=sends, recv_sem=recvs, device_id=peer, device_id_type=MESH
    )


def count_tiles(local, fan, names, store):
    rows = local.shape[0]
    local = local.astype(jnp.int16)
    one, zero = jnp.bfloat16(1), jnp.bfloat16(0)
    picked = [jnp.broadcast_to(local[:, k : k + 1], (rows, LANES)) for k in range(fan)]
    for at, columns in enumerate(names):
        columns = columns(rows)
        total = jnp.zeros((rows, LANES), jnp.bfloat16)
        for k in range(fan):
            total = total + jnp.where(picked[k] == columns, one, zero)
        store(at * LANES, total)


def plain_names(base, count):
    def name(start, rows):
        return (lax.broadcasted_iota(jnp.int32, (rows, LANES), 1) + start).astype(jnp.int16)

    return [functools.partial(name, base + at * LANES) for at in range(count)]


def main_kernel(d, names, *refs):
    r = types.SimpleNamespace(**dict(zip(names, refs)))
    f32, bf16 = jnp.float32, jnp.bfloat16
    node, feat = lax.axis_index("node"), lax.axis_index("feat")
    z, x = node // d.big_x, lax.rem(node, d.big_x)
    y, core = feat // CORES, lax.rem(feat, CORES)
    other = 1 - core
    place = core * d.big_y + y
    x_peers = [{"node": z * d.big_x + lax.rem(x + o, d.big_x)} for o in range(1, d.big_x)]
    y_peers = [{"feat": lax.rem(y + o, d.big_y) * CORES + core} for o in range(1, d.big_y)]
    z_peers = [{"node": lax.rem(z + o, d.big_z) * d.big_x + x} for o in range(1, d.big_z)]
    f_peers = [{"feat": lax.rem(feat + o, d.feats)} for o in range(1, d.feats)]
    c_peer = {"feat": y * CORES + other}
    p_peers = []
    for o in range(1, d.big_x * d.feats):
        spot = lax.rem(x * d.feats + feat + o, d.big_x * d.feats)
        p_peers.append({"node": z * d.big_x + spot // d.feats, "feat": lax.rem(spot, d.feats)})

    def z_peer(to):
        return {"node": to * d.big_x + x}

    my_rows = pl.ds(pl.multiple_of(x * d.rows, d.rows), d.rows)
    my_units = pl.ds(pl.multiple_of(feat * d.hidden_part, d.hidden_part), d.hidden_part)
    loads = [
        pltpu.make_async_copy(r.table, r.tables.at[my_rows], r.load.at[0]),
        pltpu.make_async_copy(r.self_one, r.w_self, r.load.at[1]),
        pltpu.make_async_copy(r.pool_one, r.w_pool, r.load.at[2]),
        pltpu.make_async_copy(r.self_two, r.v_self.at[my_units], r.load.at[3]),
        pltpu.make_async_copy(r.pool_two, r.v_pool.at[my_units], r.load.at[4]),
    ]
    for copy in loads:
        copy.start()
    hub_top = d.big_x * d.rows
    r.hubs[...] = jnp.zeros(r.hubs.shape, bf16)
    r.hubs[0 : d.hubs_here, :] = r.hub[...]
    r.tables[hub_top : d.depth, :] = jnp.zeros((d.depth - hub_top, d.width), bf16)
    my_hubs = pl.ds(pl.multiple_of(hub_top + x * HUB_ROWS, HUB_ROWS), HUB_ROWS)
    r.tables[my_hubs, :] = r.hubs[...]
    greet(z_peers + p_peers)

    def x_copy(h, o):
        cut = pl.ds(h * LANES, LANES)
        return remote(
            r.table.at[:, cut], r.tables.at[my_rows, cut], r.x_ss.at[h, o], r.x_rs.at[h, o], x_peers[o]
        )


    def h_copy(o):
        return remote(r.hubs, r.tables.at[my_hubs], r.h_ss.at[o], r.h_rs.at[o], x_peers[o])

    for o in range(d.big_x - 1):
        h_copy(o).start()
        x_copy(0, o).start()

    line = lax.broadcasted_iota(jnp.int32, (LIST_ROWS, d.front), 0)
    r.raw[...] = jnp.full((LIST_ROWS, d.front), -1, jnp.int32)
    r.raw[0 : d.fan_one, :] = r.lists_one[...]
    counts = jnp.broadcast_to(r.counts_one[...].reshape(1, d.front), (LIST_ROWS, d.front))
    entry = jnp.where(line < jnp.minimum(counts, d.fan_one), r.raw[...], -1)

    def decode(to):
        here = entry - to * (d.big_x * d.rows)
        found = jnp.where((here >= 0) & (here < hub_top), here, -1)
        for slot in range(d.big_x):
            hub = entry - (d.shards * d.rows + (to * d.big_x + slot) * d.hubs_here)
            found = jnp.where(
                (hub >= 0) & (hub < d.hubs_here), hub + (hub_top + slot * HUB_ROWS), found
            )
        return found

    def l_copy(o):
        to = lax.rem(z + o, d.big_z)
        return remote(
            r.l_send.at[o - 1], r.l_recv.at[z], r.l_ss.at[o - 1], r.l_rs.at[o - 1], z_peer(to)
        )

    for o in range(1, d.big_z):
        r.l_send[o - 1] = decode(lax.rem(z + o, d.big_z)).astype(jnp.int16)
        l_copy(o).start()

    def place_rows(slot, found):
        turned = found.T
        for to, start, _ in d.order:
            r.local[slot, to : to + d.step, :] = turned[start : start + d.step, :]

    own_slot = d.big_z - 1
    place_rows(own_slot, jnp.where(line == d.fan_one, counts, decode(z)))

    line_two = lax.broadcasted_iota(jnp.int32, (8, d.targets), 0)
    counts_two = jnp.broadcast_to(r.counts_two[...], (8, d.targets))
    r.raw_two[...] = jnp.full((8, d.targets), -1, jnp.int32)
    r.raw_two[0 : d.fan_two, :] = r.lists_two[...]
    second = jnp.where(line_two < jnp.minimum(counts_two, d.fan_two), r.raw_two[...], -1)
    second = jnp.where(line_two == d.fan_two, counts_two, second)
    r.s_send[...] = second
    r.s_recv[z] = second

    def s_copy(o):
        return remote(r.s_send, r.s_recv.at[z], r.s_ss.at[o], r.s_rs.at[o], z_peers[o])

    for o in range(d.big_z - 1):
        s_copy(o).start()

    for h in range(1, d.chunks):
        for o in range(d.big_x - 1):
            x_copy(h, o).start()

    def v_copies(o):
        return [
            remote(r.self_two, r.v_self.at[my_units], r.v_ss.at[0, o], r.v_rs.at[0, o], f_peers[o]),
            remote(r.pool_two, r.v_pool.at[my_units], r.v_ss.at[1, o], r.v_rs.at[1, o], f_peers[o]),
        ]

    for o in range(d.feats - 1):
        for copy in v_copies(o):
            copy.start()

    own_rows = pl.ds(pl.multiple_of(x * d.rows, d.rows), d.front)

    def own_part(j, carry):
        cut = pl.ds(pl.multiple_of(j * d.tile, LANES), d.tile)
        value = jnp.dot(r.tables[own_rows, :], r.w_self[:, cut], preferred_element_type=f32)
        for to, start, _ in d.order:
            r.part[j, to : to + d.step, :] = value[start : start + d.step, :]
        return carry

    turn = 2 * z // d.big_z

    turns = max(d.big_z - 1, 1)

    def target_of(s):
        mirrored = z + turn * (d.big_z - 1 - 2 * z)
        back = (s + mirrored) // turns
        to = (1 - back) * (d.big_z - 1 - s) + back * (s + mirrored - turns)
        return to + turn * (d.big_z - 1 - 2 * to)

    for o in range(1, d.big_z):
        l_copy(o).wait()

    def take_list(s, carry):
        place_rows(s, r.l_recv[target_of(s)].astype(jnp.int32))
        return carry

    lax.fori_loop(0, d.big_z - 1, take_list, 0)

    tile_names = plain_names(0, d.depth // LANES)

    def fill(slot):
        def group(i, carry):
            row0 = pl.multiple_of(i * 32, 32)

            def store(start, value):
                r.matrix[slot, pl.ds(row0, 32), start : start + LANES] = value

            count_tiles(r.local[slot, pl.ds(row0, 32), :], d.fan_one, tile_names, store)
            return carry

        lax.fori_loop(0, d.front // 32, group, 0)

    last = d.chunks - 1
    block = d.feats * d.step
    split = [h for h in (last - 1, last) if h > 0 or h == last]
    pieces = [(0, d.front, h) for h in range(split[0])]
    whole = len(pieces)
    piece_of = {}
    for group in (range(d.blocks - 1), (d.blocks - 1,)):
        for h in split:
            for q in group:
                piece_of[q, h] = len(pieces)
                pieces.append((q * block, block, h))
    odd = lax.rem(z, 2)
    partner = z + 1 - 2 * odd

    def region(p):
        top, deep, h = pieces[p]
        return pl.ds(top, deep), pl.ds(h * LANES, LANES)

    def held(s):
        to = target_of(s)
        return ((odd == 1) & (to > z)) | ((odd == 0) & (to < z))

    def led(s):
        to = target_of(s)
        return ((odd == 0) & (to > z + 1)) | ((odd == 1) & (to < z - 1))

    def hop_copy(s, p, slot, peer):
        rows, cut = region(p)
        return remote(
            r.z_send.at[s, rows, cut],
            r.z_recv.at[slot, rows, cut],
            r.z_ss.at[s, p],
            r.z_rs.at[slot, p],
            z_peer(peer),
        )

    def led_copy(s, p):
        return hop_copy(s, p, d.big_z + target_of(s), partner)

    def final_copy(s, p):
        return hop_copy(s, p, z, target_of(s))

    def arrival(slot, p):
        rows, cut = region(p)
        at = r.z_recv.at[slot, rows, cut]
        return remote(at, at, r.z_rs.at[slot, p], r.z_rs.at[slot, p], z_peer(lax.rem(z + 1, d.big_z)))

    def relay(p):
        top, deep, h = pieces[p]
        rows = slice(top, top + deep)
        cut = slice(h * LANES, (h + 1) * LANES)

        def one(s, carry):
            @pl.when(held(s))
            def _():
                slot = d.big_z + target_of(s)
                arrival(slot, p).wait_recv()
                r.z_send[s, rows, cut] = (
                    r.hold[s, rows, cut] + r.z_recv[slot, rows, cut].astype(f32)
                ).astype(bf16)
                final_copy(s, p).start()

            return carry

        lax.fori_loop(0, d.big_z - 1, one, 0)

    def sums(h, s):
        cut = slice(h * LANES, (h + 1) * LANES)
        value = jnp.dot(r.matrix[s], r.tables[:, cut], preferred_element_type=f32)

        kept = held(s)

        @pl.when(kept)
        def _():
            r.hold[s, :, cut] = value

        @pl.when(jnp.logical_not(kept))
        def _():
            r.z_send[s, :, cut] = value.astype(bf16)

    def launch(s, p):
        @pl.when(led(s))
        def _():
            led_copy(s, p).start()

        @pl.when(jnp.logical_not(held(s) | led(s)))
        def _():
            final_copy(s, p).start()

    def send_all(ps):
        for s in range(d.big_z - 1):
            for p in ps:
                launch(s, p)

    def chunk(h):
        for o in range(d.big_x - 1):
            x_copy(h, o).wait()

        def one_target(s, carry):
            sums(h, s)
            if h < split[0]:
                launch(s, h)
            elif last > 1:
                for q in range(d.blocks - 1):
                    launch(s, piece_of[q, h])
            return carry

        lax.fori_loop(0, d.big_z - 1, one_target, 0)

    relayed = set()

    def relays(p):
        if d.big_z > 2 and p not in relayed:
            relayed.add(p)

            relay(p)

    def fill_second(n, carry):
        local = (r.s_recv[n]).T
        r.turned[...] = local
        mine = r.turned[pl.ds(pl.multiple_of(feat * d.piece, 8), d.piece), :]
        row = pl.multiple_of(n * d.piece, 16)

        for slot in range(d.big_x):

            def store(start, value, base=slot * d.front):
                r.matrix_two[pl.ds(row, d.piece), base + start : base + start + LANES] = value

            owner = z * d.big_x + slot
            found = jnp.clip(mine[:, 0 : d.fan_two] - owner * d.front, -1, d.front)
            count_tiles(found, d.fan_two, second_names, store)
        r.scale_two[pl.ds(row, d.piece), :] = 1.0 / mine[:, d.fan_two : d.fan_two + 1].astype(f32)
        return carry

    def second_name(start, rows):
        lane = lax.broadcasted_iota(jnp.int32, (rows, LANES), 1) + start
        q = lane // block
        rest = lane - q * block
        spot = rest // d.step
        within = rest - spot * d.step
        c = spot // d.big_y
        f = (spot - c * d.big_y) * CORES + c
        early = d.targets + f * d.step + within
        late = f * d.piece + (q - 1) * d.step + within
        return jnp.where(q == 0, early, late).astype(jnp.int16)

    second_names = [functools.partial(second_name, at) for at in range(0, d.front, LANES)]

    fill(0)
    if d.big_z > 2:
        fill(1)
    for o in range(d.big_x - 1):
        x_copy(0, o).wait()
        h_copy(o).wait()
    loads[0].wait()

    def first_sums(s, carry):
        @pl.when(s > 1)
        def _():
            fill(s)

        sums(0, s)
        if split[0] > 0:
            launch(s, 0)
        return carry

    lax.fori_loop(0, d.big_z - 1, first_sums, 0)
    if last == 0:
        loads[1].wait()
        lax.fori_loop(0, TILES, own_part, 0)
    for h in range(1, d.chunks):
        if h < last - 1:
            relays(h - 1)
        if h == last and last > 1:
            relays(piece_of[0, last - 1])
        chunk(h)
        if h == 1:
            loads[1].wait()
            lax.fori_loop(0, TILES, own_part, 0)
        if h == last - 1:
            if h - 1 >= 0 and split[0] > h - 1:
                relays(h - 1)
        if h == max(last - 2, 1):
            for o in range(d.big_z - 1):
                s_copy(o).wait()
            lax.fori_loop(0, d.big_z, fill_second, 0)
        if h == last - 1:
            fill(own_slot)
    if last <= 1:
        if last == 0:
            for o in range(d.big_z - 1):
                s_copy(o).wait()
            lax.fori_loop(0, d.big_z, fill_second, 0)
        fill(own_slot)
        send_all(range(whole, len(pieces)))
    else:
        send_all([piece_of[d.blocks - 1, h] for h in split])
    def gather(p):
        top, deep, h = pieces[p]
        rows = slice(top, top + deep)
        cut = slice(h * LANES, (h + 1) * LANES)
        for o in range(1, d.big_z):
            src = lax.rem(z + o, d.big_z)
            below = (src < z) & (lax.rem(src, 2) == 1)
            above = (src > z) & (lax.rem(src, 2) == 0)

            @pl.when((src == partner) | below | above)
            def _(src=src):
                arrival(src, p).wait_recv()
                r.acc[rows, cut] += r.z_recv[src, rows, cut].astype(f32)

    rest = [piece_of[d.blocks - 1, h] for h in split]
    ahead = [piece_of[q, split[0]] for q in range(d.blocks - 1)] if len(split) > 1 else []
    for p in list(range(whole)) + ahead:
        relays(p)
    r.acc[...] = jnp.dot(r.matrix[own_slot], r.tables[...], preferred_element_type=f32)
    for p in range(whole):
        gather(p)
    for p in range(len(pieces)):
        if p not in rest:
            relays(p)
    loads[2].wait()
    half = d.big_y * d.step

    def c_copy(q, j):
        return remote(r.c_send.at[q, j], r.c_recv.at[q, j], r.c_ss.at[q, j], r.c_rs.at[q, j], c_peer)

    def y_copy(q, j, o):
        return remote(
            r.y_send.at[q, j, o], r.y_recv.at[q, j, o], r.y_ss.at[q, j, o], r.y_rs.at[q, j, o], y_peers[o]
        )

    def project(q):
        rows = slice(q * block, (q + 1) * block)
        counted = r.local[own_slot, rows, d.fan_one : d.fan_one + 1].astype(f32)
        r.means[rows, :] = (r.acc[rows, :] / counted).astype(bf16)

        def tile(j, carry):
            cut = pl.ds(pl.multiple_of(j * d.tile, LANES), d.tile)
            r.tot[...] = r.part[j, rows, :] + jnp.dot(
                r.means[rows, :], r.w_pool[:, cut], preferred_element_type=f32
            )
            far = pl.ds(pl.multiple_of(other * half, half), half)
            near = pl.ds(pl.multiple_of(core * half, half), half)
            r.c_send[q, j] = r.tot[far, :].astype(bf16)
            c_copy(q, j).start()
            r.mine[q, j] = r.tot[near, :].reshape(d.big_y, d.step, d.tile)
            return carry

        lax.fori_loop(0, TILES, tile, 0)

    def across(q):
        def tile(j, carry):
            c_copy(q, j).wait()
            r.mine[q, j] += r.c_recv[q, j].astype(f32).reshape(d.big_y, d.step, d.tile)
            for o in range(d.big_y - 1):
                r.y_send[q, j, o] = r.mine[q, j, lax.rem(y + 1 + o, d.big_y)].astype(bf16)
                y_copy(q, j, o).start()
            return carry

        lax.fori_loop(0, TILES, tile, 0)

    def proj_rows(q):
        return pl.ds(pl.multiple_of(x * d.front + q * block + place * d.step, d.step), d.step)

    def p_copy(q, o):
        at = r.proj.at[proj_rows(q)]
        return remote(at, at, r.p_ss.at[q, o], r.p_rs.at[q, o], p_peers[o])

    def finish(q):
        mine = slice(q * d.step, (q + 1) * d.step)
        for j in range(TILES):
            total = r.mine[q, j, y]
            for o in range(d.big_y - 1):
                y_copy(q, j, o).wait()
                total = total + r.y_recv[q, j, o].astype(f32)
            r.hidden[mine, j * d.tile : (j + 1) * d.tile] = jnp.maximum(total, 0.0)
        value = jnp.dot(r.hidden[mine, :].astype(bf16), r.v_pool[...], preferred_element_type=f32)
        r.proj[proj_rows(q), :] = value.astype(bf16).astype(r.proj.dtype)
        for o in range(len(p_peers)):
            p_copy(q, o).start()

    for q in range(d.blocks):
        if q == d.blocks - 2:
            relays(rest[0])
        if q == d.blocks - 1:
            for p in rest:
                relays(p)
        if q > 0:
            across(q - 1)
        for h in split:
            gather(piece_of[q, h])
        project(q)
        if q == 0:
            loads[3].wait()
            loads[4].wait()
            for o in range(d.feats - 1):
                for copy in v_copies(o):
                    copy.wait()
    for q in range(d.blocks - 2):
        finish(q)
    across(d.blocks - 1)
    for q in range(max(d.blocks - 2, 0), d.blocks):
        finish(q)
    own_two = jnp.dot(r.hidden[d.step :, :].astype(bf16), r.v_self[...], preferred_element_type=f32)
    for q in range(d.blocks):
        for o in range(len(p_peers)):
            p_copy(q, o).wait()
    r.mixed[...] = (
        jnp.dot(r.matrix_two[...], r.proj[...].astype(bf16), preferred_element_type=f32) * r.scale_two[...]
    )

    def m_copy(o):
        return remote(r.m_send.at[o], r.m_recv.at[o], r.m_ss.at[o], r.m_rs.at[o], z_peers[o])

    ways = sorted(range(d.big_z - 1), key=lambda o: abs(o + 1 - d.big_z // 2))
    for o in ways:
        to = pl.multiple_of(lax.rem(z + 1 + o, d.big_z) * d.piece, 16)
        r.m_send[o] = r.mixed[pl.ds(to, d.piece), :].astype(bf16)
        m_copy(o).start()
    total = own_two + r.mixed[pl.ds(pl.multiple_of(z * d.piece, 16), d.piece), :]
    for s in range(d.big_z - 1):
        for p in range(len(pieces)):
            final_copy(s, p).wait_send()
    for o in reversed(ways):
        m_copy(o).wait()
        total = total + r.m_recv[o].astype(f32)
    scale = lax.rsqrt(jnp.mean(total * total, axis=1, keepdims=True) + 1e-06)
    r.out[...] = (total * scale).astype(bf16)


def body(
    feature_table,
    hub_table,
    first_self,
    first_pooled,
    second_self,
    second_pooled,
    first_lists,
    first_counts,
    second_lists,
    second_counts,
):
    d = types.SimpleNamespace()
    d.shards = lax.axis_size("node")
    d.feats = lax.axis_size("feat")
    d.big_x = 2 ** ((d.shards.bit_length() - 1) // 2)
    d.big_z = d.shards // d.big_x
    d.big_y = d.feats // CORES
    d.rows, d.width = feature_table.shape
    d.hubs_here = hub_table.shape[0]
    d.front, d.fan_one = first_lists.shape
    d.targets, d.fan_two = second_lists.shape
    d.piece = d.targets // d.feats
    d.out_width = second_self.shape[1]
    d.hidden_part = second_self.shape[0]
    units = d.hidden_part * d.feats
    d.tile = units // TILES
    d.depth = d.big_x * d.rows + -(-d.big_x * HUB_ROWS // LANES) * LANES
    d.chunks = d.width // LANES
    d.step = (d.front - d.targets) // d.feats
    d.blocks = d.front // (d.step * d.feats)
    assert d.step * d.feats * d.blocks == d.front and d.piece % d.step == 0
    order = []
    for q in range(d.blocks):
        for c in range(CORES):
            for yy in range(d.big_y):
                f = yy * CORES + c
                start = d.targets + f * d.step if q == 0 else f * d.piece + (q - 1) * d.step
                order.append((q * d.step * d.feats + (c * d.big_y + yy) * d.step, start, f))
    d.order = order
    bf16, f32, i32, i16 = jnp.bfloat16, jnp.float32, jnp.int32, jnp.int16
    dma, vm = pltpu.SemaphoreType.DMA, pltpu.VMEM
    zs, xs, ys, fs = d.big_z - 1, d.big_x - 1, d.big_y - 1, d.feats - 1
    count = d.chunks * d.blocks
    half = d.big_y * d.step
    kind = bf16 if d.step % 16 == 0 else f32
    scratch = dict(
        tables=vm((d.depth, d.width), bf16),
        w_self=vm((d.width, units), bf16),
        w_pool=vm((d.width, units), bf16),
        v_self=vm((units, d.out_width), bf16),
        v_pool=vm((units, d.out_width), bf16),
        hubs=vm((HUB_ROWS, d.width), bf16),
        raw=vm((LIST_ROWS, d.front), i32),
        raw_two=vm((8, d.targets), i32),
        l_send=vm((zs, LIST_ROWS, d.front), i16),
        l_recv=vm((d.big_z, LIST_ROWS, d.front), i16),
        s_send=vm((8, d.targets), i32),
        s_recv=vm((d.big_z, 8, d.targets), i32),
        turned=vm((d.targets, 8), i32),
        local=vm((d.big_z, d.front, LIST_ROWS), i32),
        matrix=vm((d.big_z, d.front, d.depth), bf16),
        matrix_two=vm((d.big_z * d.piece, d.big_x * d.front), bf16),
        scale_two=vm((d.big_z * d.piece, 1), f32),
        part=vm((TILES, d.front, d.tile), f32),
        hold=vm((zs, d.front, d.width), f32),
        z_send=vm((zs, d.front, d.width), bf16),
        z_recv=vm((2 * d.big_z, d.front, d.width), bf16),
        acc=vm((d.front, d.width), f32),
        means=vm((d.front, d.width), bf16),
        tot=vm((d.step * d.feats, d.tile), f32),
        mine=vm((d.blocks, TILES, d.big_y, d.step, d.tile), f32),
        c_send=vm((d.blocks, TILES, half, d.tile), bf16),
        c_recv=vm((d.blocks, TILES, half, d.tile), bf16),
        y_send=vm((d.blocks, TILES, ys, d.step, d.tile), bf16),
        y_recv=vm((d.blocks, TILES, ys, d.step, d.tile), bf16),
        hidden=vm((d.blocks * d.step, units), f32),
        proj=vm((d.big_x * d.front, d.out_width), kind),
        mixed=vm((d.big_z * d.piece, d.out_width), f32),
        m_send=vm((zs, d.piece, d.out_width), bf16),
        m_recv=vm((zs, d.piece, d.out_width), bf16),
        load=dma((5,)),
        x_ss=dma((d.chunks, xs)),
        x_rs=dma((d.chunks, xs)),
        h_ss=dma((xs,)),
        h_rs=dma((xs,)),
        l_ss=dma((zs,)),
        l_rs=dma((zs,)),
        s_ss=dma((zs,)),
        s_rs=dma((zs,)),
        v_ss=dma((2, fs)),
        v_rs=dma((2, fs)),
        z_ss=dma((zs, count)),
        z_rs=dma((2 * d.big_z, count)),
        c_ss=dma((d.blocks, TILES)),
        c_rs=dma((d.blocks, TILES)),
        y_ss=dma((d.blocks, TILES, ys)),
        y_rs=dma((d.blocks, TILES, ys)),
        p_ss=dma((d.blocks, d.big_x * d.feats - 1)),
        p_rs=dma((d.blocks, d.big_x * d.feats - 1)),
        m_ss=dma((zs,)),
        m_rs=dma((zs,)),
    )
    inputs = ["table", "hub", "self_one", "pool_one", "self_two", "pool_two"]
    inputs += ["lists_one", "counts_one", "lists_two", "counts_two"]
    names = inputs + ["out"] + list(scratch)
    vmem = pl.BlockSpec(memory_space=pltpu.VMEM)
    hbm = pl.BlockSpec(memory_space=pl.ANY)
    return pl.pallas_call(
        functools.partial(main_kernel, d, names),
        out_shape=jax.ShapeDtypeStruct((d.piece, d.out_width), bf16),
        in_specs=[hbm, vmem, hbm, hbm, hbm, hbm, vmem, vmem, vmem, vmem],
        out_specs=vmem,
        scratch_shapes=list(scratch.values()),
        compiler_params=pltpu.CompilerParams(
            collective_id=1, has_side_effects=True, vmem_limit_bytes=60 * 1024 * 1024
        ),
    )(
        feature_table,
        hub_table,
        first_self,
        first_pooled,
        second_self,
        second_pooled,
        first_lists.T,
        first_counts,
        second_lists.T,
        second_counts[None, :],
    )


def solution(mesh):
    return jax.shard_map(
        body,
        mesh=mesh,
        in_specs=(
            P("node", "feat"),
            P("node", "feat"),
            P("feat", None),
            P("feat", None),
            P("feat", None),
            P("feat", None),
            P("node", None),
            P("node"),
            P("node", None),
            P("node"),
        ),
        out_specs=P(("node", "feat"), None),
        check_vma=False,
    )
```
